32 devices in a mesh: nodes: 8 (over z, x), dp: 4 (over y, core).
Axes of the slice: x: 2, y: 2, z: 4, core: 2. Of those that a mesh axis runs over, the one named last changes fastest.
Arguments:
- samples: float32 [16384, 256], P('dp'), may hold values from -96 to 96, as said below
- basis_matrix: float32 [8192, 4096], P('nodes', 'dp'), may hold values from 0 to 0.03
- weights: float32 [4096, 256], P('dp'), may hold values from -12 to 12, as said below
Outputs:
- new_weights: float32 [4096, 256], P('dp')
- new_centres: float32 [8192, 256], P('nodes')
The draws below stay inside these ranges and needn't reach their ends.
Inputs may be any that keep to these rules, and one draw needn't show every extreme that they name: `samples`: finite data values. `weights`: finite weight values.
All inputs are finite; a program needn't handle non-finite values.
Results may differ from the reference program's by a relative error of at most 0.0003.
Values sent between devices are 32-bit elements; how exact they have to be, the bound alone decides.
A program may use at most 64 MiB of HBM per device.

```python
import math
import jax
import jax.numpy as jnp
from jax import lax

D = 256
M = 4096
KDEV = 1024
K = 8192
N = 16384


def draw_samples(key, part):
    first_key = jax.random.fold_in(jax.random.fold_in(key, 7), 0)
    mask_key, level_key, noise_key = jax.random.split(jax.random.fold_in(key, 13), 3)
    values = jnp.clip(jax.random.normal(first_key, (N, D), jnp.float32), -6.0, 6.0)
    picked = jax.random.uniform(mask_key, (N, 1), jnp.float32) < 0.125
    picked = jnp.logical_or(picked, (jnp.arange(N) == 0)[:, None])
    levels = jax.random.uniform(level_key, (N, 1), jnp.float32, 0.55, 1.0)
    strong = jnp.clip(84.0 * levels + 2.0 * jax.random.normal(noise_key, (N, D), jnp.float32), -96.0, 96.0)
    columns = (jnp.arange(D) < 4)[None, :]
    return jnp.where(jnp.logical_and(picked, columns), strong, values)


def draw_weights(key, part):
    weight_key = jax.random.fold_in(key, 11)
    values = jnp.clip(jax.random.normal(weight_key, (M, D), jnp.float32), -6.0, 6.0)
    values = values - jnp.mean(values, axis=0, keepdims=True)
    shared = jnp.where(jnp.arange(D) < 4, 8.0 / (0.015 * M), 0.0)
    return values + shared[None, :]


def block_scale(rng, extent, cuts, smallest, top_value):
    loudness = 1.0
    for axis_at, shards_of in cuts:
        heights = jax.random.uniform(jax.random.fold_in(jax.random.fold_in(rng, 6), axis_at), (shards_of,), jnp.float32, smallest / len(cuts), top_value / len(cuts))
        loudness = loudness * jnp.repeat(jnp.exp(heights), extent[axis_at] // shards_of).reshape((-1,) + (1,) * (len(extent) - 1 - axis_at))
    return loudness


def setup_inputs(seed: int = 0) -> dict:
    arg_keys = jax.random.split(jax.random.key(seed), 4)
    return {
        "samples": draw_samples(jax.random.fold_in(arg_keys[3], 71), 0),
        "basis_matrix": jnp.clip(0.03 * jax.random.uniform(arg_keys[1], (K, M), jnp.float32) ** block_scale(arg_keys[1], (K, M), ((0, 8), (1, 4)), -0.2, 0.2), 0.0, 0.03),
        "weights": draw_weights(jax.random.fold_in(arg_keys[3], 71), 0),
    }


highest = lax.Precision.HIGHEST
inverse_temp = 0.25
shrink = 0.95

def node_scores(centre_block, samples):
    cross = lax.dot_general(centre_block, samples, (((1,), (1,)), ((), ())), precision=highest, preferred_element_type=jnp.float32)
    return inverse_temp * (cross - 0.5 * lax.optimization_barrier(jnp.sum(centre_block * centre_block, axis=1))[:, None])

def reference(samples, basis_matrix, weights):
    centres = jnp.dot(basis_matrix, weights, precision=highest, preferred_element_type=jnp.float32)
    blocks = centres.reshape(K // KDEV, KDEV, D)

    def update(running, centre_block):
        maxima, totals = running
        scores = node_scores(centre_block, samples)
        merged = jnp.maximum(maxima, lax.optimization_barrier(jnp.max(scores, axis=0)))
        totals = totals * jnp.exp(maxima - merged) + lax.optimization_barrier(jnp.sum(jnp.exp(scores - merged[None, :]), axis=0))
        return ((merged, totals), None)
    start = (jnp.full((N,), -jnp.inf, jnp.float32), jnp.zeros((N,), jnp.float32))
    (maxima, totals), _ = lax.scan(update, start, blocks)

    def terms(centre_block):
        resp = jnp.exp(node_scores(centre_block, samples) - maxima[None, :]) / totals[None, :]
        weighted = jnp.dot(resp, samples, precision=highest, preferred_element_type=jnp.float32)
        return lax.optimization_barrier(jnp.sum(resp, axis=1))[:, None] * centre_block - weighted
    node_terms = lax.map(terms, blocks).reshape(K, D)
    gradient = lax.dot_general(basis_matrix, node_terms, (((0,), (0,)), ((), ())), precision=highest, preferred_element_type=jnp.float32)
    step_rate = 8.0 * math.sqrt(K) / N
    new_weights = shrink * weights - step_rate * gradient
    new_centres = jnp.dot(basis_matrix, new_weights, precision=highest, preferred_element_type=jnp.float32)
    return (new_weights, new_centres)
```

```python
import functools
import math

import jax
import jax.numpy as jnp
from jax import lax
from jax.experimental import pallas as pl
from jax.experimental.pallas import tpu as pltpu
from jax.sharding import PartitionSpec as P

f32 = jnp.float32
bf16 = jnp.bfloat16
MESH = pl.DeviceIdType.MESH
shrink = 0.95
CH = 4
VC = 512


def split(a):
    hi = a.astype(bf16)
    return hi, (a - hi.astype(f32)).astype(bf16)


def dot(a, b, trans_b=False):
    dims = (((1,), (1 if trans_b else 0,)), ((), ()))
    return lax.dot_general(a, b, dims, preferred_element_type=f32)


def dot3(ah, al, bh, bl, trans_b=False):
    return dot(ah, bh, trans_b) + (dot(ah, bl, trans_b) + dot(al, bh, trans_b))


def kernel(
    nn, nd, rate,
    x_hbm, b_hbm, w_ref, nw_hbm, nc_hbm,
    xv, bv, xh, xl, bh, bl, bth, btl, wh, wl,
    part, cent, land_c, land_y,
    bias, ex, st, st_in, fac,
    grad, lx1, lz1, lx2, lz2, nw, nc,
    lsem, ssem, rsem, st_s, st_r, g_s, g_r,
):
    kk, mm = bv.shape
    nv, d = xv.shape
    node = lax.axis_index("nodes")
    dp = lax.axis_index("dp")
    core = lax.rem(dp, 2)
    yy = dp // 2
    ny = nd // 2
    xx = lax.rem(node, 2)
    zz = node // 2
    nz = nn // 2
    tk = kk // CH
    half = tk // 2
    extra = 8

    b_cp = []
    for i in range(CH):
        rows = pl.ds(i * tk, tk)
        cp = pltpu.make_async_copy(b_hbm.at[rows], bv.at[rows], lsem.at[i])
        cp.start()
        b_cp.append(cp)
    x_cp = pltpu.make_async_copy(x_hbm, xv, lsem.at[CH])
    x_cp.start()

    bar = pltpu.get_barrier_semaphore()
    partner = (node, yy * 2 + (1 - core))
    y_peers = [(node, lax.rem(yy + r, ny) * 2 + core) for r in range(1, ny)]
    n_peers = [(lax.rem(node + r, nn), dp) for r in range(1, nn)]
    for peer in [partner] + y_peers + n_peers:
        pl.semaphore_signal(bar, inc=1, device_id=peer, device_id_type=MESH)
    pl.semaphore_wait(bar, 1 + len(y_peers) + len(n_peers))

    def remote(src, dst, s, r, peer):
        cp = pltpu.make_async_remote_copy(
            src_ref=src, dst_ref=dst, send_sem=s, recv_sem=r,
            device_id=peer, device_id_type=MESH,
        )
        cp.start()
        return cp

    class Reduce:
        def __init__(self, which, out, chunks):
            self.w, self.out, self.chunks = which, out, chunks
            self.rs, self.ys, self.ag = {}, {}, {}

        def rows(self, i, c):
            base, h = self.chunks[i]
            return pl.ds(pl.multiple_of(base + c * h, 8), h)

        def lrows(self, i):
            base, h = self.chunks[i]
            return pl.ds(base // 2, h)

        def start(self, i):
            w = self.w
            self.rs[i] = remote(
                part.at[w, self.rows(i, 1 - core)], land_c.at[w, self.lrows(i)],
                ssem.at[w, 0, i], rsem.at[w, 0, i], partner,
            )

        def across(self, i):
            w = self.w
            self.rs[i].wait_recv()
            mine = self.rows(i, core)
            part[w, mine] = part[w, mine] + land_c[w, self.lrows(i)]
            self.ys[i] = [
                remote(
                    part.at[w, mine], land_y.at[w, r, self.lrows(i)],
                    ssem.at[w, 1 + r, i], rsem.at[w, 1 + r, i], peer,
                )
                for r, peer in enumerate(y_peers)
            ]

        def back(self, i):
            w = self.w
            mine = self.rows(i, core)
            total = part[w, mine]
            for r, cp in enumerate(self.ys[i]):
                cp.wait_recv()
                total = total + land_y[w, r, self.lrows(i)]
            self.out[mine] = total
            self.ag[i] = remote(
                self.out.at[mine], self.out.at[mine],
                ssem.at[w, ny, i], rsem.at[w, ny, i], partner,
            )

        def finish(self, i):
            self.ag[i].wait_recv()

        def drain(self):
            for i in self.rs:
                self.rs[i].wait_send()
                for cp in self.ys[i]:
                    cp.wait_send()
                self.ag[i].wait_send()

    plain = [(i * tk, half) for i in range(CH)]

    red = Reduce(0, cent, plain + [(kk, extra)])
    w = w_ref[...]
    hi, lo = split(w)
    wh[...] = hi
    wl[...] = lo
    part[0, pl.ds(kk, 2 * extra)] = jnp.broadcast_to(
        0.015 * jnp.sum(w, axis=0, keepdims=True), (2 * extra, d)
    )
    red.start(CH)
    for i in range(CH):
        rows = pl.ds(i * tk, tk)
        b_cp[i].wait()
        hi, lo = split(bv[rows])
        bh[rows] = hi
        bl[rows] = lo
        part[0, rows] = dot3(hi, lo, wh[...], wl[...])
        red.start(i)
    order = [CH] + list(range(CH))
    for i in order:
        red.across(i)
    x_cp.wait()

    def split_x(t, _):
        rows = pl.ds(pl.multiple_of(t * VC, VC), VC)
        h, l = split(xv[rows])
        xh[rows] = h
        xl[rows] = l
        return 0

    lax.fori_loop(0, nv // VC, split_x, 0)

    def turn(t, _):
        rows = pl.ds(pl.multiple_of(t * 128, 128), 128)
        h, l = split(jnp.transpose(bv[:, rows]))
        bth[rows] = h
        btl[rows] = l
        return 0

    lax.fori_loop(0, mm // 128, turn, 0)
    for i in order:
        red.back(i)
    for i in order:
        red.finish(i)
    red.drain()

    c0 = cent[pl.ds(kk, 1)]
    for i in range(CH):
        rows = pl.ds(i * tk, tk)
        c = cent[rows]
        bias[rows] = -0.125 * jnp.sum(c * c, axis=1, keepdims=True)
        hi, lo = split(0.25 * (c - c0))
        wh[rows] = hi
        wl[rows] = lo

    nj = nv // VC

    def scores(j, _):
        cols = pl.ds(pl.multiple_of(j * VC, VC), VC)
        top = None
        for i in range(CH):
            rows = pl.ds(i * tk, tk)
            s = dot3(wh[rows], wl[rows], xh[cols], xl[cols], True) + bias[rows]
            ex[rows, cols] = s
            m = jnp.max(s, axis=0, keepdims=True)
            top = m if top is None else jnp.maximum(top, m)
        tot = jnp.zeros_like(top)
        for i in range(CH):
            rows = pl.ds(i * tk, tk)
            e = jnp.exp(ex[rows, cols] - top)
            ex[rows, cols] = e
            tot = tot + jnp.sum(e, axis=0, keepdims=True)
        st[pl.ds(j, 1)] = top
        st[pl.ds(nj + j, 1)] = tot
        return 0

    lax.fori_loop(0, nj, scores, 0)
    st_cp = [
        remote(st, st_in.at[r], st_s.at[r], st_r.at[r], peer)
        for r, peer in enumerate(n_peers)
    ]
    mine = st[pl.ds(0, nj)]
    top, tot = mine, st[pl.ds(nj, nj)]
    for r, cp in enumerate(st_cp):
        cp.wait_recv()
        m, t = st_in[r, pl.ds(0, nj)], st_in[r, pl.ds(nj, nj)]
        new = jnp.maximum(top, m)
        tot = tot * jnp.exp(top - new) + t * jnp.exp(m - new)
        top = new
    fac[...] = jnp.exp(mine - top) / tot

    red2 = Reduce(1, nc, plain)
    for i in range(CH):
        rows = pl.ds(i * tk, tk)

        def terms(j, carry):
            acc, rs = carry
            cols = pl.ds(pl.multiple_of(j * VC, VC), VC)
            r = ex[rows, cols] * fac[pl.ds(j, 1)]
            h, l = split(r)
            acc = acc + dot3(h, l, xh[cols], xl[cols])
            for q in range(VC // 128):
                rs = rs + r[:, q * 128:(q + 1) * 128]
            return acc, rs

        acc, rs = lax.fori_loop(
            0, nj, terms, (jnp.zeros((tk, d), f32), jnp.zeros((tk, 128), f32))
        )
        part[1, rows] = jnp.sum(rs, axis=1, keepdims=True) * cent[rows] - acc
        red2.start(i)
    for i in range(CH):
        red2.across(i)
    for i in range(CH):
        red2.back(i)
    for i in range(CH):
        red2.finish(i)
        rows = pl.ds(i * tk, tk)
        hi, lo = split(nc[rows])
        wh[rows] = hi
        wl[rows] = lo
    red2.drain()

    def gradient(t, _):
        rows = pl.ds(pl.multiple_of(t * 256, 256), 256)
        grad[rows] = dot3(bth[rows], btl[rows], wh[...], wl[...])
        return 0

    h1 = lx1.shape[0]
    p1 = lz1.shape[1]
    p2 = lz2.shape[1]
    g2 = 2 * h1
    other_x = (zz * 2 + (1 - xx), dp)
    z_to = [lax.rem(zz + r, nz) for r in range(1, nz)]
    z_dev = [(t * 2 + xx, dp) for t in z_to]
    sems = iter(range(g_s.shape[0]))
    sent = []

    def ship(src, dst, peer):
        q = next(sems)
        cp = remote(src, dst, g_s.at[q], g_r.at[q], peer)
        sent.append(cp)
        return cp

    def at(start, size):
        return pl.ds(pl.multiple_of(start, 8), size)

    def update(rows, g):
        nw[rows] = shrink * w_ref[rows] - rate * g

    lax.fori_loop(0, mm // 256, gradient, 0)
    a1 = ship(grad.at[at((1 - xx) * h1, h1)], lx1, other_x)
    b1 = [
        ship(grad.at[at(g2 + t * p2, p2)], lz2.at[r], dev)
        for r, (t, dev) in enumerate(zip(z_to, z_dev))
    ]
    keep1 = at(xx * h1, h1)
    a1.wait_recv()
    grad[keep1] = grad[keep1] + lx1[...]
    a2 = [
        ship(grad.at[at(xx * h1 + t * p1, p1)], lz1.at[r], dev)
        for r, (t, dev) in enumerate(zip(z_to, z_dev))
    ]
    own2 = at(g2 + zz * p2, p2)
    total = grad[own2]
    for r, cp in enumerate(b1):
        cp.wait_recv()
        total = total + lz2[r]
    grad[own2] = total
    b2 = ship(grad.at[own2], lx2, other_x)
    own1 = at(xx * h1 + zz * p1, p1)
    total = grad[own1]
    for r, cp in enumerate(a2):
        cp.wait_recv()
        total = total + lz1[r]
    update(own1, total)
    a3 = [ship(nw.at[own1], nw.at[own1], dev) for dev in z_dev]
    b2.wait_recv()
    update(own2, grad[own2] + lx2[...])
    b3 = [ship(nw.at[own2], nw.at[own2], dev) for dev in z_dev]
    for cp in a3:
        cp.wait_recv()
    a4 = ship(nw.at[keep1], nw.at[keep1], other_x)
    for cp in b3:
        cp.wait_recv()
    a4.wait_recv()
    nw_cp = pltpu.make_async_copy(nw, nw_hbm, lsem.at[0])
    nw_cp.start()
    hi, lo = split(nw[...])
    wh[...] = hi
    wl[...] = lo

    red3 = Reduce(2, cent, plain)
    for i in range(CH):
        rows = pl.ds(i * tk, tk)
        part[2, rows] = dot3(bh[rows], bl[rows], wh[...], wl[...])
        red3.start(i)
    for i in range(CH):
        red3.across(i)
    for i in range(CH):
        red3.back(i)
    out_cp = []
    for i in range(CH):
        red3.finish(i)
        rows = pl.ds(i * tk, tk)
        cp = pltpu.make_async_copy(cent.at[rows], nc_hbm.at[rows], lsem.at[1 + i])
        cp.start()
        out_cp.append(cp)
    red3.drain()
    for cp in sent + st_cp:
        cp.wait_send()
    nw_cp.wait()
    for cp in out_cp:
        cp.wait()


def body(samples, basis_matrix, weights):
    nn, nd = lax.axis_size("nodes"), lax.axis_size("dp")
    nv, d = samples.shape
    kk, mm = basis_matrix.shape
    rate = 8.0 * math.sqrt(kk * nn) / (nv * nd)
    ny, nz = nd // 2, nn // 2
    nj = nv // VC
    h1 = mm // 4
    n_ship = 3 + 4 * (nz - 1)
    vm = pltpu.VMEM
    dma = pltpu.SemaphoreType.DMA
    anyspec = pl.BlockSpec(memory_space=pl.ANY)
    return pl.pallas_call(
        functools.partial(kernel, nn, nd, rate),
        out_shape=(
            jax.ShapeDtypeStruct((mm, d), f32),
            jax.ShapeDtypeStruct((kk, d), f32),
        ),
        in_specs=[anyspec, anyspec, pl.BlockSpec(memory_space=pltpu.VMEM)],
        out_specs=(anyspec, anyspec),
        scratch_shapes=[
            vm((nv, d), f32), vm((kk, mm), f32),
            vm((nv, d), bf16), vm((nv, d), bf16),
            vm((kk, mm), bf16), vm((kk, mm), bf16),
            vm((mm, kk), bf16), vm((mm, kk), bf16),
            vm((max(kk, mm), d), bf16), vm((max(kk, mm), d), bf16),
            vm((3, kk + 16, d), f32), vm((kk + 16, d), f32),
            vm((3, kk // 2 + 8, d), f32), vm((3, ny - 1, kk // 2 + 8, d), f32),
            vm((kk, 1), f32), vm((kk, nv), f32),
            vm((2 * nj, VC), f32), vm((nn - 1, 2 * nj, VC), f32), vm((nj, VC), f32),
            vm((mm, d), f32),
            vm((h1, d), f32), vm((nz - 1, h1 // nz, d), f32),
            vm((2 * h1 // nz, d), f32), vm((nz - 1, 2 * h1 // nz, d), f32),
            vm((mm, d), f32), vm((kk, d), f32),
            dma((CH + 1,)),
            dma((3, ny + 1, CH + 1)), dma((3, ny + 1, CH + 1)),
            dma((nn - 1,)), dma((nn - 1,)),
            dma((n_ship,)), dma((n_ship,)),
        ],
        compiler_params=pltpu.CompilerParams(
            collective_id=0, has_side_effects=True, vmem_limit_bytes=64000000
        ),
    )(samples, basis_matrix, weights)


def solution(mesh):
    in_specs = (P("dp", None), P("nodes", "dp"), P("dp", None))
    out_specs = (P("dp", None), P("nodes", None))
    return jax.shard_map(body, mesh=mesh, in_specs=in_specs, out_specs=out_specs, check_vma=False)
```

```python
import functools
import math

import jax
import jax.numpy as jnp
from jax import lax
from jax.experimental import pallas as pl
from jax.experimental.pallas import tpu as pltpu
from jax.sharding import PartitionSpec as P

f32 = jnp.float32
bf16 = jnp.bfloat16
MESH = pl.DeviceIdType.MESH
shrink = 0.95
CH = 4
VC = 512


def split(a):
    hi = a.astype(bf16)
    return hi, (a - hi.astype(f32)).astype(bf16)


def dot(a, b, trans_b=False):
    dims = (((1,), (1 if trans_b else 0,)), ((), ()))
    return lax.dot_general(a, b, dims, preferred_element_type=f32)


def dot3(ah, al, bh, bl, trans_b=False):
    return dot(ah, bh, trans_b) + (dot(ah, bl, trans_b) + dot(al, bh, trans_b))


def kernel(
    nn, nd, rate,
    x_hbm, b_hbm, w_hbm, nw_hbm, nc_hbm,
    w_ref, xv, bv, xh, xl, bh, bl, bth, btl, wh, wl,
    part, cent, land_c, land_y,
    bias, ex, st, st_in, fac,
    grad, lx1, lx2, lz2, nw, nc,
    lin, lmid,
    lsem, ssem, rsem, st_s, st_r, g_s, g_r, c_s, c_r,
):
    kk, mm = bv.shape
    nv, d = xv.shape
    node = lax.axis_index("nodes")
    dp = lax.axis_index("dp")
    core = lax.rem(dp, 2)
    yy = dp // 2
    ny = nd // 2
    xx = lax.rem(node, 2)
    zz = node // 2
    nz = nn // 2
    tk = kk // CH
    half = tk // 2
    extra = 8

    w_cp = pltpu.make_async_copy(w_hbm, w_ref, lsem.at[CH + 1])
    w_cp.start()
    b_cp = []
    for i in range(CH):
        rows = pl.ds(i * tk, tk)
        cp = pltpu.make_async_copy(b_hbm.at[rows], bv.at[rows], lsem.at[i])
        cp.start()
        b_cp.append(cp)
    x_cp = pltpu.make_async_copy(x_hbm, xv, lsem.at[CH])
    x_cp.start()

    bar = pltpu.get_barrier_semaphore()
    partner = (node, yy * 2 + (1 - core))
    y_peers = [(node, lax.rem(yy + r, ny) * 2 + core) for r in range(1, ny)]
    n_peers = [(lax.rem(node + r, nn), dp) for r in range(1, nn)]
    for peer in [partner] + y_peers + n_peers:
        pl.semaphore_signal(bar, inc=1, device_id=peer, device_id_type=MESH)
    pl.semaphore_wait(bar, 1 + len(y_peers) + len(n_peers))

    def remote(src, dst, s, r, peer):
        cp = pltpu.make_async_remote_copy(
            src_ref=src, dst_ref=dst, send_sem=s, recv_sem=r,
            device_id=peer, device_id_type=MESH,
        )
        cp.start()
        return cp

    class Reduce:
        def __init__(self, which, out, chunks):
            self.w, self.out, self.chunks = which, out, chunks
            self.rs, self.ys, self.ag = {}, {}, {}

        def rows(self, i, c):
            base, h = self.chunks[i]
            return pl.ds(pl.multiple_of(base + c * h, 8), h)

        def lrows(self, i):
            base, h = self.chunks[i]
            return pl.ds(base // 2, h)

        def start(self, i):
            w = self.w
            self.rs[i] = remote(
                part.at[w, self.rows(i, 1 - core)], land_c.at[w, self.lrows(i)],
                ssem.at[w, 0, i], rsem.at[w, 0, i], partner,
            )

        def across(self, i):
            w = self.w
            self.rs[i].wait_recv()
            mine = self.rows(i, core)
            part[w, mine] = part[w, mine] + land_c[w, self.lrows(i)]
            self.ys[i] = [
                remote(
                    part.at[w, mine], land_y.at[w, r, self.lrows(i)],
                    ssem.at[w, 1 + r, i], rsem.at[w, 1 + r, i], peer,
                )
                for r, peer in enumerate(y_peers)
            ]

        def back(self, i):
            w = self.w
            mine = self.rows(i, core)
            total = part[w, mine]
            for r, cp in enumerate(self.ys[i]):
                cp.wait_recv()
                total = total + land_y[w, r, self.lrows(i)]
            self.out[mine] = total
            self.ag[i] = remote(
                self.out.at[mine], self.out.at[mine],
                ssem.at[w, ny, i], rsem.at[w, ny, i], partner,
            )

        def finish(self, i):
            self.ag[i].wait_recv()

        def drain(self):
            for i in self.rs:
                self.rs[i].wait_send()
                for cp in self.ys[i]:
                    cp.wait_send()
                self.ag[i].wait_send()

    plain = [(i * tk, half) for i in range(CH)]

    red = Reduce(0, cent, plain + [(kk, extra)])
    w_cp.wait()
    w = w_ref[...]
    hi, lo = split(w)
    wh[...] = hi
    wl[...] = lo
    part[0, pl.ds(kk, 2 * extra)] = jnp.broadcast_to(
        0.015 * jnp.sum(w, axis=0, keepdims=True), (2 * extra, d)
    )
    red.start(CH)
    for i in range(CH):
        rows = pl.ds(i * tk, tk)
        b_cp[i].wait()
        hi, lo = split(bv[rows])
        bh[rows] = hi
        bl[rows] = lo
        part[0, rows] = dot3(hi, lo, wh[...], wl[...])
        red.start(i)
        red.across(CH if i == 0 else i - 1)
    order = [CH] + list(range(CH))
    red.across(CH - 1)
    x_cp.wait()

    def split_x(t, _):
        rows = pl.ds(pl.multiple_of(t * VC, VC), VC)
        h, l = split(xv[rows])
        xh[rows] = h
        xl[rows] = l
        return 0

    lax.fori_loop(0, nv // VC, split_x, 0)

    def turn(t, _):
        rows = pl.ds(pl.multiple_of(t * 128, 128), 128)
        h, l = split(jnp.transpose(bv[:, rows]))
        bth[rows] = h
        btl[rows] = l
        return 0

    lax.fori_loop(0, mm // 128, turn, 0)
    for i in order:
        red.back(i)
    for i in order:
        red.finish(i)
    red.drain()

    c0 = cent[pl.ds(kk, 1)]
    for i in range(CH):
        rows = pl.ds(i * tk, tk)
        c = cent[rows]
        bias[rows] = -0.125 * jnp.sum(c * c, axis=1, keepdims=True)
        hi, lo = split(0.25 * (c - c0))
        wh[rows] = hi
        wl[rows] = lo

    nj = nv // VC

    def scores(j, _):
        cols = pl.ds(pl.multiple_of(j * VC, VC), VC)
        top = None
        for i in range(CH):
            rows = pl.ds(i * tk, tk)
            s = dot3(wh[rows], wl[rows], xh[cols], xl[cols], True) + bias[rows]
            ex[rows, cols] = s
            m = jnp.max(s, axis=0, keepdims=True)
            top = m if top is None else jnp.maximum(top, m)
        tot = jnp.zeros_like(top)
        for i in range(CH):
            rows = pl.ds(i * tk, tk)
            e = jnp.exp(ex[rows, cols] - top)
            ex[rows, cols] = e
            tot = tot + jnp.sum(e, axis=0, keepdims=True)
        st[pl.ds(j, 1)] = top
        st[pl.ds(nj + j, 1)] = tot
        return 0

    lax.fori_loop(0, nj, scores, 0)
    st_cp = [
        remote(st, st_in.at[r], st_s.at[r], st_r.at[r], peer)
        for r, peer in enumerate(n_peers)
    ]
    mine = st[pl.ds(0, nj)]
    top, tot = mine, st[pl.ds(nj, nj)]
    for r, cp in enumerate(st_cp):
        cp.wait_recv()
        m, t = st_in[r, pl.ds(0, nj)], st_in[r, pl.ds(nj, nj)]
        new = jnp.maximum(top, m)
        tot = tot * jnp.exp(top - new) + t * jnp.exp(m - new)
        top = new
    fac[...] = jnp.exp(mine - top) / tot

    red2 = Reduce(1, nc, plain)
    for i in range(CH):
        rows = pl.ds(i * tk, tk)

        def terms(j, carry):
            acc, rs = carry
            cols = pl.ds(pl.multiple_of(j * VC, VC), VC)
            r = ex[rows, cols] * fac[pl.ds(j, 1)]
            h, l = split(r)
            acc = acc + dot3(h, l, xh[cols], xl[cols])
            for q in range(VC // 128):
                rs = rs + r[:, q * 128:(q + 1) * 128]
            return acc, rs

        acc, rs = lax.fori_loop(
            0, nj, terms, (jnp.zeros((tk, d), f32), jnp.zeros((tk, 128), f32))
        )
        part[1, rows] = jnp.sum(rs, axis=1, keepdims=True) * cent[rows] - acc
        red2.start(i)
        if i:
            red2.across(i - 1)
    red2.across(CH - 1)
    for i in range(CH):
        red2.back(i)
    for i in range(CH):
        red2.finish(i)
        rows = pl.ds(i * tk, tk)
        hi, lo = split(nc[rows])
        wh[rows] = hi
        wl[rows] = lo
    red2.drain()

    def gradient(start, size):
        rows = pl.ds(start, size)
        grad[rows] = dot3(bth[rows], btl[rows], wh[...], wl[...])

    nc1, hc = lx1.shape[0], lx1.shape[1]
    p2 = lz2.shape[1]
    g2 = nc1 * 2 * hc
    mid = nz // 2
    left = zz < mid
    is_mid = jnp.logical_or(zz == mid - 1, zz == mid)
    not_mid = jnp.logical_not(is_mid)
    is_end = jnp.logical_or(zz == 0, zz == nz - 1)
    not_end = jnp.logical_not(is_end)
    step = jnp.where(left, 1, -1)
    inner = (lax.rem(zz + step + nz, nz) * 2 + xx, dp)
    outer = (lax.rem(zz - step + nz, nz) * 2 + xx, dp)
    other_x = (zz * 2 + (1 - xx), dp)
    z_to = [lax.rem(zz + r, nz) for r in range(1, nz)]
    z_dev = [(t * 2 + xx, dp) for t in z_to]
    sems = iter(range(g_s.shape[0]))
    sent = []

    def ship(src, dst, peer):
        q = next(sems)
        cp = remote(src, dst, g_s.at[q], g_r.at[q], peer)
        sent.append(cp)
        return cp

    def at(start, size):
        return pl.ds(pl.multiple_of(start, 8), size)

    def update(rows, g):
        nw[rows] = shrink * w_ref[rows] - rate * g

    def plan(src, dst, kind, c, peer):
        return pltpu.make_async_remote_copy(
            src_ref=src, dst_ref=dst, send_sem=c_s.at[kind, c], recv_sem=c_r.at[kind, c],
            device_id=peer, device_id_type=MESH,
        )

    gradient(g2, mm - g2)
    b1 = [
        ship(grad.at[at(g2 + t * p2, p2)], lz2.at[r], dev)
        for r, (t, dev) in enumerate(zip(z_to, z_dev))
    ]
    keep = [at((2 * c + xx) * hc, hc) for c in range(nc1)]
    give = [at((2 * c + 1 - xx) * hc, hc) for c in range(nc1)]
    x_rs, x_ag = [], {}
    inward = [plan(grad.at[keep[c]], lin.at[c], 0, c, inner) for c in range(nc1)]
    swap = [plan(grad.at[keep[c]], lmid.at[c], 1, c, inner) for c in range(nc1)]
    outward = [plan(nw.at[keep[c]], nw.at[keep[c]], 2, c, outer) for c in range(nc1)]
    for c in range(nc1):
        gradient(2 * c * hc, 2 * hc)
        x_rs.append(ship(grad.at[give[c]], lx1.at[c], other_x))

    def stage0(c):
        x_rs[c].wait_recv()
        grad[keep[c]] = grad[keep[c]] + lx1[c]

        @pl.when(jnp.logical_and(is_end, not_mid))
        def _():
            inward[c].start()

    def stage1(c):
        @pl.when(not_end)
        def _():
            inward[c].wait_recv()
            grad[keep[c]] = grad[keep[c]] + lin[c]

        @pl.when(jnp.logical_and(not_end, not_mid))
        def _():
            inward[c].start()

        @pl.when(is_mid)
        def _():
            swap[c].start()

    def stage2(c):
        @pl.when(is_mid)
        def _():
            swap[c].wait_recv()
            update(keep[c], grad[keep[c]] + lmid[c])

        @pl.when(jnp.logical_and(is_mid, not_end))
        def _():
            outward[c].start()

    def stage3(c):
        @pl.when(not_mid)
        def _():
            outward[c].wait_recv()

        @pl.when(jnp.logical_and(not_mid, not_end))
        def _():
            outward[c].start()

        x_ag[c] = ship(nw.at[keep[c]], nw.at[keep[c]], other_x)

    own2 = at(g2 + zz * p2, p2)
    for t in range(nc1 + 3):
        if t < nc1:
            stage0(t)
        if 0 <= t - 1 < nc1:
            stage1(t - 1)
        if 0 <= t - 2 < nc1:
            stage2(t - 2)
        if 0 <= t - 3 < nc1:
            stage3(t - 3)
        if t == 2:
            total = grad[own2]
            for r, cp in enumerate(b1):
                cp.wait_recv()
                total = total + lz2[r]
            grad[own2] = total
            b2 = ship(grad.at[own2], lx2, other_x)
        if t == 4:
            b2.wait_recv()
            update(own2, grad[own2] + lx2[...])
            b3 = [ship(nw.at[own2], nw.at[own2], dev) for dev in z_dev]
    for cp in b3:
        cp.wait_recv()
    for c in range(nc1):
        x_ag[c].wait_recv()

        @pl.when(not_mid)
        def _():
            inward[c].wait_send()

        @pl.when(is_mid)
        def _():
            swap[c].wait_send()

        @pl.when(not_end)
        def _():
            outward[c].wait_send()

    nw_cp = pltpu.make_async_copy(nw, nw_hbm, lsem.at[0])
    nw_cp.start()
    hi, lo = split(nw[...])
    wh[...] = hi
    wl[...] = lo

    red3 = Reduce(2, cent, plain)
    for i in range(CH):
        rows = pl.ds(i * tk, tk)
        part[2, rows] = dot3(bh[rows], bl[rows], wh[...], wl[...])
        red3.start(i)
        if i:
            red3.across(i - 1)
    red3.across(CH - 1)
    for i in range(CH):
        red3.back(i)
    out_cp = []
    for i in range(CH):
        red3.finish(i)
        rows = pl.ds(i * tk, tk)
        cp = pltpu.make_async_copy(cent.at[rows], nc_hbm.at[rows], lsem.at[1 + i])
        cp.start()
        out_cp.append(cp)
    red3.drain()
    for cp in sent + st_cp:
        cp.wait_send()
    nw_cp.wait()
    for cp in out_cp:
        cp.wait()


def body(samples, basis_matrix, weights):
    nn, nd = lax.axis_size("nodes"), lax.axis_size("dp")
    nv, d = samples.shape
    kk, mm = basis_matrix.shape
    rate = 8.0 * math.sqrt(kk * nn) / (nv * nd)
    ny, nz = nd // 2, nn // 2
    nj = nv // VC
    nc1 = 6
    hc = mm // 16
    g2 = mm - 2 * nc1 * hc
    n_ship = 2 * nc1 + 1 + 2 * (nz - 1)
    vm = pltpu.VMEM
    dma = pltpu.SemaphoreType.DMA
    anyspec = pl.BlockSpec(memory_space=pl.ANY)
    return pl.pallas_call(
        functools.partial(kernel, nn, nd, rate),
        out_shape=(
            jax.ShapeDtypeStruct((mm, d), f32),
            jax.ShapeDtypeStruct((kk, d), f32),
        ),
        in_specs=[anyspec, anyspec, anyspec],
        out_specs=(anyspec, anyspec),
        scratch_shapes=[
            vm((mm, d), f32), vm((nv, d), f32), vm((kk, mm), f32),
            vm((nv, d), bf16), vm((nv, d), bf16),
            vm((kk, mm), bf16), vm((kk, mm), bf16),
            vm((mm, kk), bf16), vm((mm, kk), bf16),
            vm((max(kk, mm), d), bf16), vm((max(kk, mm), d), bf16),
            vm((3, kk + 16, d), f32), vm((kk + 16, d), f32),
            vm((3, kk // 2 + 8, d), f32), vm((3, ny - 1, kk // 2 + 8, d), f32),
            vm((kk, 1), f32), vm((kk, nv), f32),
            vm((2 * nj, VC), f32), vm((nn - 1, 2 * nj, VC), f32), vm((nj, VC), f32),
            vm((mm, d), f32),
            vm((nc1, hc, d), f32), vm((g2 // nz, d), f32), vm((nz - 1, g2 // nz, d), f32),
            vm((mm, d), f32), vm((kk, d), f32),
            vm((nc1, hc, d), f32), vm((nc1, hc, d), f32),
            dma((CH + 2,)),
            dma((3, ny + 1, CH + 1)), dma((3, ny + 1, CH + 1)),
            dma((nn - 1,)), dma((nn - 1,)),
            dma((n_ship,)), dma((n_ship,)), dma((3, nc1)), dma((3, nc1)),
        ],
        compiler_params=pltpu.CompilerParams(
            collective_id=0, has_side_effects=True, vmem_limit_bytes=64000000
        ),
    )(samples, basis_matrix, weights)


def solution(mesh):
    in_specs = (P("dp", None), P("nodes", "dp"), P("dp", None))
    out_specs = (P("dp", None), P("nodes", None))
    return jax.shard_map(body, mesh=mesh, in_specs=in_specs, out_specs=out_specs, check_vma=False)
```

```python
import functools
import math

import jax
import jax.numpy as jnp
from jax import lax
from jax.experimental import pallas as pl
from jax.experimental.pallas import tpu as pltpu
from jax.sharding import PartitionSpec as P

f32 = jnp.float32
bf16 = jnp.bfloat16
MESH = pl.DeviceIdType.MESH
shrink = 0.95
CH = 4
VC = 512
LAG = 2
EARLY = 2


def split(a):
    hi = a.astype(bf16)
    return hi, (a - hi.astype(f32)).astype(bf16)


def dot(a, b, trans_b=False):
    dims = (((1,), (1 if trans_b else 0,)), ((), ()))
    return lax.dot_general(a, b, dims, preferred_element_type=f32)


def dot3(ah, al, bh, bl, trans_b=False):
    return dot(ah, bh, trans_b) + (dot(ah, bl, trans_b) + dot(al, bh, trans_b))


def kernel(
    nn, nd, rate,
    x_hbm, b_hbm, w_hbm, nw_hbm, nc_hbm,
    w_ref, xv, bv, xh, xl, bh, bl, bth, btl, wh, wl,
    part, cent, land_c, land_y,
    bias, ex, st, st_in, fac,
    grad, lx1, lx2, lz2, nw, nc,
    lin, lmid, rsum,
    lsem, ssem, rsem, st_s, st_r, g_s, g_r, c_s, c_r,
):
    kk, mm = bv.shape
    nv, d = xv.shape
    node = lax.axis_index("nodes")
    dp = lax.axis_index("dp")
    core = lax.rem(dp, 2)
    yy = dp // 2
    ny = nd // 2
    xx = lax.rem(node, 2)
    zz = node // 2
    nz = nn // 2
    tk = kk // CH
    half = tk // 2
    extra = 8

    w_cp = pltpu.make_async_copy(w_hbm, w_ref, lsem.at[CH + 1])
    w_cp.start()
    b_cp = []
    for i in range(CH):
        rows = pl.ds(i * tk, tk)
        cp = pltpu.make_async_copy(b_hbm.at[rows], bv.at[rows], lsem.at[i])
        cp.start()
        b_cp.append(cp)
    x_cp = pltpu.make_async_copy(x_hbm, xv, lsem.at[CH])
    x_cp.start()

    bar = pltpu.get_barrier_semaphore()
    partner = (node, yy * 2 + (1 - core))
    y_peers = [(node, lax.rem(yy + r, ny) * 2 + core) for r in range(1, ny)]
    n_peers = [(lax.rem(node + r, nn), dp) for r in range(1, nn)]
    for peer in [partner] + y_peers + n_peers:
        pl.semaphore_signal(bar, inc=1, device_id=peer, device_id_type=MESH)

    def remote(src, dst, s, r, peer):
        cp = pltpu.make_async_remote_copy(
            src_ref=src, dst_ref=dst, send_sem=s, recv_sem=r,
            device_id=peer, device_id_type=MESH,
        )
        cp.start()
        return cp

    class Reduce:
        def __init__(self, which, out, chunks):
            self.w, self.out, self.chunks = which, out, chunks
            self.rs, self.ys, self.ag = {}, {}, {}

        def rows(self, i, c):
            base, h = self.chunks[i]
            return pl.ds(pl.multiple_of(base + c * h, 8), h)

        def lrows(self, i):
            base, h = self.chunks[i]
            return pl.ds(base // 2, h)

        def start(self, i):
            w = self.w
            self.rs[i] = remote(
                part.at[w, self.rows(i, 1 - core)], land_c.at[w, self.lrows(i)],
                ssem.at[w, 0, i], rsem.at[w, 0, i], partner,
            )

        def across(self, i):
            w = self.w
            self.rs[i].wait_recv()
            mine = self.rows(i, core)
            part[w, mine] = part[w, mine] + land_c[w, self.lrows(i)]
            self.ys[i] = [
                remote(
                    part.at[w, mine], land_y.at[w, r, self.lrows(i)],
                    ssem.at[w, 1 + r, i], rsem.at[w, 1 + r, i], peer,
                )
                for r, peer in enumerate(y_peers)
            ]

        def back(self, i):
            w = self.w
            mine = self.rows(i, core)
            total = part[w, mine]
            for r, cp in enumerate(self.ys[i]):
                cp.wait_recv()
                total = total + land_y[w, r, self.lrows(i)]
            self.out[mine] = total
            self.ag[i] = remote(
                self.out.at[mine], self.out.at[mine],
                ssem.at[w, ny, i], rsem.at[w, ny, i], partner,
            )

        def finish(self, i):
            self.ag[i].wait_recv()

        def drain(self):
            for i in self.rs:
                self.rs[i].wait_send()
                for cp in self.ys[i]:
                    cp.wait_send()
                self.ag[i].wait_send()

    plain = [(i * tk, half) for i in range(CH)]

    red = Reduce(0, cent, plain + [(kk, extra)])
    w_cp.wait()
    w = w_ref[...]
    hi, lo = split(w)
    wh[...] = hi
    wl[...] = lo
    part[0, pl.ds(kk, 2 * extra)] = jnp.broadcast_to(
        0.015 * jnp.sum(w, axis=0, keepdims=True), (2 * extra, d)
    )
    for i in range(CH):
        rows = pl.ds(i * tk, tk)
        b_cp[i].wait()
        hi, lo = split(bv[rows])
        bh[rows] = hi
        bl[rows] = lo
        part[0, rows] = dot3(hi, lo, wh[...], wl[...])
        if i == 0:
            pl.semaphore_wait(bar, 1 + len(y_peers) + len(n_peers))
            red.start(CH)
        red.start(i)
        red.across(CH if i == 0 else i - 1)
    order = [CH] + list(range(CH))
    red.across(CH - 1)
    x_cp.wait()

    def split_x(t, _):
        rows = pl.ds(pl.multiple_of(t * VC, VC), VC)
        h, l = split(xv[rows])
        xh[rows] = h
        xl[rows] = l
        return 0

    lax.fori_loop(0, nv // VC, split_x, 0)

    def turn(t, _):
        rows = pl.ds(pl.multiple_of(t * 128, 128), 128)
        h, l = split(jnp.transpose(bv[:, rows]))
        bth[rows] = h
        btl[rows] = l
        return 0

    lax.fori_loop(0, mm // 128, turn, 0)
    for i in order:
        red.back(i)
    for i in order:
        red.finish(i)
    red.drain()

    c0 = cent[pl.ds(kk, 1)]
    for i in range(CH):
        rows = pl.ds(i * tk, tk)
        c = cent[rows]
        bias[rows] = -0.125 * jnp.sum(c * c, axis=1, keepdims=True)
        hi, lo = split(0.25 * (c - c0))
        wh[rows] = hi
        wl[rows] = lo

    njh = st.shape[1] // 2

    def scores(g, j):
        cols = pl.ds(pl.multiple_of((g * njh + j) * VC, VC), VC)
        top = None
        for i in range(CH):
            rows = pl.ds(i * tk, tk)
            s = dot3(wh[rows], wl[rows], xh[cols], xl[cols], True) + bias[rows]
            ex[rows, cols] = s
            m = jnp.max(s, axis=0, keepdims=True)
            top = m if top is None else jnp.maximum(top, m)
        tot = jnp.zeros_like(top)
        for i in range(CH):
            rows = pl.ds(i * tk, tk)
            e = jnp.exp(ex[rows, cols] - top)
            ex[rows, cols] = e
            tot = tot + jnp.sum(e, axis=0, keepdims=True)
        st[g, pl.ds(j, 1)] = top
        st[g, pl.ds(njh + j, 1)] = tot

    st_cp = []
    for g in range(2):

        def scores_g(j, _):
            scores(g, j)
            return 0

        lax.fori_loop(0, njh, scores_g, 0)
        st_cp += [
            remote(st.at[g], st_in.at[g, r], st_s.at[g, r], st_r.at[g, r], peer)
            for r, peer in enumerate(n_peers)
        ]

    def merge(g):
        mine = st[g, pl.ds(0, njh)]
        top, tot = mine, st[g, pl.ds(njh, njh)]
        for r in range(nn - 1):
            st_cp[g * (nn - 1) + r].wait_recv()
            m, t = st_in[g, r, pl.ds(0, njh)], st_in[g, r, pl.ds(njh, njh)]
            new = jnp.maximum(top, m)
            tot = tot * jnp.exp(top - new) + t * jnp.exp(m - new)
            top = new
        fac[g] = jnp.exp(mine - top) / tot

    red2 = Reduce(1, nc, plain)

    def terms(i, g, start):
        rows = pl.ds(i * tk, tk)

        def one(j, carry):
            acc, rs = carry
            cols = pl.ds(pl.multiple_of((g * njh + j) * VC, VC), VC)
            r = ex[rows, cols] * fac[g, pl.ds(j, 1)]
            h, l = split(r)
            acc = acc + dot3(h, l, xh[cols], xl[cols])
            for q in range(VC // 128):
                rs = rs + r[:, q * 128:(q + 1) * 128]
            return acc, rs

        return lax.fori_loop(0, njh, one, start, unroll=2)

    zero = (jnp.zeros((tk, d), f32), jnp.zeros((tk, 128), f32))
    merge(0)
    for i in range(EARLY):
        rows = pl.ds(i * tk, tk)
        acc, rs = terms(i, 0, zero)
        grad[rows] = acc
        rsum[rows] = rs
    merge(1)
    for i in range(CH):
        rows = pl.ds(i * tk, tk)
        first = (grad[rows], rsum[rows]) if i < EARLY else terms(i, 0, zero)
        acc, rs = terms(i, 1, first)
        part[1, rows] = jnp.sum(rs, axis=1, keepdims=True) * cent[rows] - acc
        red2.start(i)
        if i:
            red2.across(i - 1)
    red2.across(CH - 1)
    for i in range(CH):
        red2.back(i)
    for i in range(CH):
        red2.finish(i)
        rows = pl.ds(i * tk, tk)
        hi, lo = split(nc[rows])
        wh[rows] = hi
        wl[rows] = lo
    red2.drain()

    def gradient(start, size):
        rows = pl.ds(start, size)
        grad[rows] = dot3(bth[rows], btl[rows], wh[...], wl[...])

    nc1, hc = lx1.shape[0], lx1.shape[1]
    p2 = lz2.shape[1]
    g2 = nc1 * 2 * hc
    mid = nz // 2
    left = zz < mid
    is_mid = jnp.logical_or(zz == mid - 1, zz == mid)
    not_mid = jnp.logical_not(is_mid)
    is_end = jnp.logical_or(zz == 0, zz == nz - 1)
    not_end = jnp.logical_not(is_end)
    step = jnp.where(left, 1, -1)
    inner = (lax.rem(zz + step + nz, nz) * 2 + xx, dp)
    outer = (lax.rem(zz - step + nz, nz) * 2 + xx, dp)
    other_x = (zz * 2 + (1 - xx), dp)
    z_to = [lax.rem(zz + r, nz) for r in range(1, nz)]
    z_dev = [(t * 2 + xx, dp) for t in z_to]
    sems = iter(range(g_s.shape[0]))
    sent = []

    def ship(src, dst, peer):
        q = next(sems)
        cp = remote(src, dst, g_s.at[q], g_r.at[q], peer)
        sent.append(cp)
        return cp

    def at(start, size):
        return pl.ds(pl.multiple_of(start, 8), size)

    def update(rows, g):
        nw[rows] = shrink * w_ref[rows] - rate * g

    def plan(src, dst, kind, c, peer):
        return pltpu.make_async_remote_copy(
            src_ref=src, dst_ref=dst, send_sem=c_s.at[kind, c], recv_sem=c_r.at[kind, c],
            device_id=peer, device_id_type=MESH,
        )

    gradient(g2, mm - g2)
    b1 = [
        ship(grad.at[at(g2 + t * p2, p2)], lz2.at[r], dev)
        for r, (t, dev) in enumerate(zip(z_to, z_dev))
    ]
    keep = [at((2 * c + xx) * hc, hc) for c in range(nc1)]
    give = [at((2 * c + 1 - xx) * hc, hc) for c in range(nc1)]
    x_rs, x_ag = [], {}
    inward = [plan(grad.at[keep[c]], lin.at[c], 0, c, inner) for c in range(nc1)]
    swap = [plan(grad.at[keep[c]], lmid.at[c], 1, c, inner) for c in range(nc1)]
    outward = [plan(nw.at[keep[c]], nw.at[keep[c]], 2, c, outer) for c in range(nc1)]
    for c in range(nc1):
        gradient(2 * c * hc, 2 * hc)
        x_rs.append(ship(grad.at[give[c]], lx1.at[c], other_x))

    def stage0(c):
        x_rs[c].wait_recv()
        grad[keep[c]] = grad[keep[c]] + lx1[c]

        @pl.when(jnp.logical_and(is_end, not_mid))
        def _():
            inward[c].start()

    def stage1(c):
        @pl.when(not_end)
        def _():
            inward[c].wait_recv()
            grad[keep[c]] = grad[keep[c]] + lin[c]

        @pl.when(jnp.logical_and(not_end, not_mid))
        def _():
            inward[c].start()

        @pl.when(is_mid)
        def _():
            swap[c].start()

    def stage2(c):
        @pl.when(is_mid)
        def _():
            swap[c].wait_recv()
            update(keep[c], grad[keep[c]] + lmid[c])

        @pl.when(jnp.logical_and(is_mid, not_end))
        def _():
            outward[c].start()

    def stage3(c):
        @pl.when(not_mid)
        def _():
            outward[c].wait_recv()

        @pl.when(jnp.logical_and(not_mid, not_end))
        def _():
            outward[c].start()

        x_ag[c] = ship(nw.at[keep[c]], nw.at[keep[c]], other_x)

    own2 = at(g2 + zz * p2, p2)
    for t in range(nc1 + 3 * LAG):
        for n, stage in enumerate((stage0, stage1, stage2, stage3)):
            if 0 <= t - n * LAG < nc1:
                stage(t - n * LAG)
        if t == 3:
            total = grad[own2]
            for r, cp in enumerate(b1):
                cp.wait_recv()
                total = total + lz2[r]
            grad[own2] = total
            b2 = ship(grad.at[own2], lx2, other_x)
        if t == 6:
            b2.wait_recv()
            update(own2, grad[own2] + lx2[...])
            b3 = [ship(nw.at[own2], nw.at[own2], dev) for dev in z_dev]
    for cp in b3:
        cp.wait_recv()
    for c in range(nc1):
        x_ag[c].wait_recv()

        @pl.when(not_mid)
        def _():
            inward[c].wait_send()

        @pl.when(is_mid)
        def _():
            swap[c].wait_send()

        @pl.when(not_end)
        def _():
            outward[c].wait_send()

    nw_cp = pltpu.make_async_copy(nw, nw_hbm, lsem.at[0])
    nw_cp.start()
    hi, lo = split(nw[...])
    wh[...] = hi
    wl[...] = lo

    red3 = Reduce(2, cent, plain)
    for i in range(CH):
        rows = pl.ds(i * tk, tk)
        part[2, rows] = dot3(bh[rows], bl[rows], wh[...], wl[...])
        red3.start(i)
        if i:
            red3.across(i - 1)
    red3.across(CH - 1)
    for i in range(CH):
        red3.back(i)
    out_cp = []
    for i in range(CH):
        red3.finish(i)
        rows = pl.ds(i * tk, tk)
        cp = pltpu.make_async_copy(cent.at[rows], nc_hbm.at[rows], lsem.at[1 + i])
        cp.start()
        out_cp.append(cp)
    red3.drain()
    for cp in sent + st_cp:
        cp.wait_send()
    nw_cp.wait()
    for cp in out_cp:
        cp.wait()


def body(samples, basis_matrix, weights):
    nn, nd = lax.axis_size("nodes"), lax.axis_size("dp")
    nv, d = samples.shape
    kk, mm = basis_matrix.shape
    rate = 8.0 * math.sqrt(kk * nn) / (nv * nd)
    ny, nz = nd // 2, nn // 2
    nj = nv // VC
    nc1 = 6
    hc = mm // 16
    g2 = mm - 2 * nc1 * hc
    n_ship = 2 * nc1 + 1 + 2 * (nz - 1)
    vm = pltpu.VMEM
    dma = pltpu.SemaphoreType.DMA
    anyspec = pl.BlockSpec(memory_space=pl.ANY)
    return pl.pallas_call(
        functools.partial(kernel, nn, nd, rate),
        out_shape=(
            jax.ShapeDtypeStruct((mm, d), f32),
            jax.ShapeDtypeStruct((kk, d), f32),
        ),
        in_specs=[anyspec, anyspec, anyspec],
        out_specs=(anyspec, anyspec),
        scratch_shapes=[
            vm((mm, d), f32), vm((nv, d), f32), vm((kk, mm), f32),
            vm((nv, d), bf16), vm((nv, d), bf16),
            vm((kk, mm), bf16), vm((kk, mm), bf16),
            vm((mm, kk), bf16), vm((mm, kk), bf16),
            vm((max(kk, mm), d), bf16), vm((max(kk, mm), d), bf16),
            vm((3, kk + 16, d), f32), vm((kk + 16, d), f32),
            vm((3, kk // 2 + 8, d), f32), vm((3, ny - 1, kk // 2 + 8, d), f32),
            vm((kk, 1), f32), vm((kk, nv), f32),
            vm((2, nj, VC), f32), vm((2, nn - 1, nj, VC), f32), vm((2, nj // 2, VC), f32),
            vm((max(mm, kk), d), f32),
            vm((nc1, hc, d), f32), vm((g2 // nz, d), f32), vm((nz - 1, g2 // nz, d), f32),
            vm((mm, d), f32), vm((kk, d), f32),
            vm((nc1, hc, d), f32), vm((nc1, hc, d), f32), vm((kk, 128), f32),
            dma((CH + 2,)),
            dma((3, ny + 1, CH + 1)), dma((3, ny + 1, CH + 1)),
            dma((2, nn - 1)), dma((2, nn - 1)),
            dma((n_ship,)), dma((n_ship,)), dma((3, nc1)), dma((3, nc1)),
        ],
        compiler_params=pltpu.CompilerParams(
            collective_id=0, has_side_effects=True, vmem_limit_bytes=64000000
        ),
    )(samples, basis_matrix, weights)


def solution(mesh):
    in_specs = (P("dp", None), P("nodes", "dp"), P("dp", None))
    out_specs = (P("dp", None), P("nodes", None))
    return jax.shard_map(body, mesh=mesh, in_specs=in_specs, out_specs=out_specs, check_vma=False)
```
